128 devices in a mesh: pipe: 4 (over y_lo, core), expert: 32 (over x, z, y_hi).
Axes of the slice: x: 4, y: 4 (y_hi: 2, y_lo: 2; y = y_hi * 2 + y_lo), z: 4, core: 2. Of those that a mesh axis runs over, the one named last changes fastest.
Arguments:
- next_input: bfloat16 [4, 8192, 2048], P('pipe', 'expert'), may hold values from -6 to 6
- prev_input: bfloat16 [4, 8192, 2048], P('pipe', 'expert'), may hold values from -6 to 6
- next_cot: bfloat16 [4, 8192, 2048], P('pipe', 'expert'), may hold values from -6 to 6
- gate_weight: bfloat16 [4, 32, 2048, 768], P('pipe', 'expert'), may hold values from -0.125 to 0.125
- up_weight: bfloat16 [4, 32, 2048, 768], P('pipe', 'expert'), may hold values from -0.125 to 0.125
- down_weight: bfloat16 [4, 32, 768, 2048], P('pipe', 'expert'), may hold values from -0.21875 to 0.21875
- router: bfloat16 [4, 2048, 32], P('pipe'), may hold values from -0.125 to 0.125
- gain: float32 [4, 2048], P('pipe'), may hold values from 0.1 to 1.9
- next_routes: int32 [4, 8192, 2], P('pipe', 'expert'), may hold values from 0 to 31, all different within a row
- prev_routes: int32 [4, 8192, 2], P('pipe', 'expert'), may hold values from 0 to 31, all different within a row
- next_priority: int32 [4, 8192], P('pipe', 'expert'), may hold values from 0 to 8191, each once within a row
- prev_priority: int32 [4, 8192], P('pipe', 'expert'), may hold values from 0 to 8191, each once within a row
Outputs:
- forward_out: bfloat16 [4, 8192, 2048], P('pipe', 'expert')
- input_grad: bfloat16 [4, 8192, 2048], P('pipe', 'expert')
- gate_grad: bfloat16 [4, 32, 2048, 768], P('pipe', 'expert')
- up_grad: bfloat16 [4, 32, 2048, 768], P('pipe', 'expert')
- down_grad: bfloat16 [4, 32, 768, 2048], P('pipe', 'expert')
- router_grad: float32 [4, 2048, 32], P('pipe')
- gain_grad: float32 [4, 2048], P('pipe')
The draws below stay inside these ranges and needn't reach their ends.
All inputs are finite; a program needn't handle non-finite values.
Results may differ from the reference program's by a relative error of at most 0.0085.
Values may be sent and summed in bfloat16 or wider, within the bound.
A program may use at most 128 MiB of HBM per device.

```python
import jax
import jax.numpy as jnp
from jax import lax

D = 2048
FF = 768
TOP = 2
TOK_DEV = 256
EXPERTS = 32
TOKENS = 8192
CAP = 20
N_PIPE = 4
N_EXPERT = 32


def steps_of(key, extent, split, least, top_value):
    level, own = 1.0, jax.random.fold_in(key, 6)
    for position, shards_of in split:
        draws = jnp.exp(jax.random.uniform(jax.random.fold_in(own, position), (shards_of,), jnp.float32, least / len(split), top_value / len(split)))
        level = level * jnp.repeat(draws, extent[position] // shards_of).reshape([-1 if axis == position else 1 for axis in range(len(extent))])
    return level


def different_ones(own_key, rows, amount, top, lift):
    ranking = jax.random.permutation(jax.random.fold_in(own_key, 1), amount)
    boost = ranking
    for power in range(3):
        boost = boost * boost // amount
    boost = boost * lift // amount
    lots = jax.random.randint(jax.random.fold_in(own_key, 2), (rows, amount), 0, 4096) + boost
    sure = jax.random.permutation(jax.random.fold_in(own_key, 3), rows)[jnp.arange(amount) % rows]
    lots = jnp.where(jnp.arange(rows)[:, None] == sure[None, :], 1 << 14, lots)
    score = lots * amount + jnp.arange(amount)
    return lax.top_k(score.astype(jnp.int32), top)[1].astype(jnp.int32)


def noise(own_key, extent, scale, limit, pieces=(), held_as=jnp.bfloat16):
    values = jax.random.normal(own_key, extent, jnp.float32) * scale
    if len(pieces) > 0:
        values = steps_of(own_key, extent, pieces, -0.22, 0.18) * values
    return jnp.clip(values, min=-limit, max=limit).astype(held_as)


def setup_inputs(seed: int = 0) -> dict:
    keys = jax.random.split(jax.random.key(seed), 13)
    return {
        "next_input": noise(keys[0], (N_PIPE, TOKENS, D), 1.0, 6.0, ((0, 4), (1, 32))),
        "prev_input": noise(keys[1], (N_PIPE, TOKENS, D), 1.0, 6.0, ((0, 4), (1, 32))),
        "next_cot": noise(keys[2], (N_PIPE, TOKENS, D), 1.0, 6.0, ((0, 4), (1, 32))),
        "gate_weight": noise(keys[3], (N_PIPE, EXPERTS, D, FF), D ** -0.5, 0.125, ((0, 4), (1, 32))),
        "up_weight": noise(keys[4], (N_PIPE, EXPERTS, D, FF), D ** -0.5, 0.125, ((0, 4), (1, 32))),
        "down_weight": noise(keys[5], (N_PIPE, EXPERTS, FF, D), FF ** -0.5, 0.21875, ((0, 4), (1, 32))),
        "router": noise(keys[6], (N_PIPE, D, EXPERTS), D ** -0.5, 0.125, ((0, 4),)),
        "gain": jnp.clip(1.0 + 0.18 * jax.random.normal(keys[7], (N_PIPE, D), jnp.float32), 0.1, 1.9),
        "next_routes": different_ones(keys[8], N_PIPE * TOKENS, EXPERTS, TOP, 1024).reshape((N_PIPE, TOKENS, TOP)),
        "prev_routes": different_ones(keys[9], N_PIPE * TOKENS, EXPERTS, TOP, 1024).reshape((N_PIPE, TOKENS, TOP)),
        "next_priority": jax.vmap(lambda own: jax.random.permutation(own, TOKENS))(jax.random.split(keys[10], N_PIPE)).reshape((N_PIPE, TOKENS)).astype(jnp.int32),
        "prev_priority": jax.vmap(lambda own: jax.random.permutation(own, TOKENS))(jax.random.split(keys[11], N_PIPE)).reshape((N_PIPE, TOKENS)).astype(jnp.int32),
    }


EPS = 1e-06

def rms_scaled(values, gain):
    scale = lax.rsqrt(lax.optimization_barrier(jnp.mean(values * values, axis=-1, keepdims=True)) + EPS)
    return values * scale * gain

def pair_weights(selected):
    lifted = jax.nn.sigmoid(selected)
    return lifted / lax.optimization_barrier(jnp.sum(lifted, axis=-1, keepdims=True))

def slot_table(routes, priority, experts, capacity):
    top = routes.shape[1]
    picks = routes.reshape(-1).astype(jnp.int32)
    order = jnp.repeat(priority, top)
    same = picks[:, None] == picks[None, :]
    before = order[None, :] < order[:, None]
    rank = lax.optimization_barrier(jnp.sum(jnp.where(same & before, 1, 0), axis=1)).astype(jnp.int32)
    kept = rank < capacity
    slots = jnp.where(kept, picks * capacity + rank, experts * capacity).astype(jnp.int32)
    match = slots[None, :] == jnp.arange(experts * capacity, dtype=jnp.int32)[:, None]
    filled = jnp.any(match, axis=1)
    source = lax.optimization_barrier(jnp.sum(jnp.where(match, jnp.arange(picks.shape[0], dtype=jnp.int32)[None, :], 0), axis=1)).astype(jnp.int32)
    return (slots, filled, source)

def prepare(section_in, gain, router, routes, priority, capacity):
    experts = router.shape[-1]
    top = routes.shape[1]
    values = section_in.astype(jnp.float32)
    normed = rms_scaled(values, gain).astype(jnp.bfloat16)
    logits = jnp.dot(normed.astype(jnp.float32), router.astype(jnp.float32), preferred_element_type=jnp.float32)
    selected = jnp.take_along_axis(logits, routes, axis=1)
    slots, filled, source = slot_table(routes, priority, experts, capacity)
    token = source // top
    rows = jnp.where(filled[:, None], normed[token], jnp.zeros_like(normed[token]))
    rows = rows.reshape(experts, capacity, normed.shape[1])
    return (values, normed, selected, slots, filled, source, rows)

def pick_rows(table, slots):
    flat = table.reshape(-1, table.shape[-1])
    padded = jnp.concatenate([flat, jnp.zeros((1, flat.shape[1]), flat.dtype)], axis=0)
    return padded[slots].astype(jnp.float32)

def combine(values, selected, slots, produced):
    top = selected.shape[1]
    weights = pair_weights(selected).reshape(-1, 1)
    taken = pick_rows(produced, slots) * weights
    total = lax.optimization_barrier(jnp.sum(taken.reshape(values.shape[0], top, values.shape[1]), axis=1))
    return (values + total).astype(jnp.bfloat16)

def as_wide(array):
    return array.astype(jnp.float32)

def expert_forward(shaped, gate_w, up_w, down_w):
    gate = jnp.einsum('secd,edf->secf', as_wide(shaped), as_wide(gate_w))
    upper = jnp.einsum('secd,edf->secf', as_wide(shaped), as_wide(up_w))
    active = (gate * jax.nn.sigmoid(gate) * upper).astype(jnp.bfloat16)
    return jnp.einsum('secf,efd->secd', as_wide(active), as_wide(down_w)).astype(jnp.bfloat16)

def expert_backward(shaped, cot, scales, gate_w, up_w, down_w):
    gate = jnp.einsum('secd,edf->secf', as_wide(shaped), as_wide(gate_w))
    upper = jnp.einsum('secd,edf->secf', as_wide(shaped), as_wide(up_w))
    sig = jax.nn.sigmoid(gate)
    lifted = gate * sig
    active = (lifted * upper).astype(jnp.bfloat16)
    result = jnp.einsum('secf,efd->secd', as_wide(active), as_wide(down_w)).astype(jnp.bfloat16)
    inner = lax.optimization_barrier(jnp.sum(cot.astype(jnp.float32) * result.astype(jnp.float32), axis=-1, keepdims=True)).astype(jnp.bfloat16)
    scaled = (scales.astype(jnp.float32) * cot.astype(jnp.float32)).astype(jnp.bfloat16)
    down_part = jnp.einsum('secf,secd->efd', as_wide(active), as_wide(scaled))
    act_grad = jnp.einsum('secd,efd->secf', as_wide(scaled), as_wide(down_w))
    gate_part = (act_grad * upper * sig * (1.0 + gate * (1.0 - sig))).astype(jnp.bfloat16)
    up_part = (act_grad * lifted).astype(jnp.bfloat16)
    gate_wgrad = jnp.einsum('secd,secf->edf', as_wide(shaped), as_wide(gate_part))
    up_wgrad = jnp.einsum('secd,secf->edf', as_wide(shaped), as_wide(up_part))
    row_grad = jnp.einsum('secf,edf->secd', as_wide(gate_part), as_wide(gate_w))
    row_grad = (row_grad + jnp.einsum('secf,edf->secd', as_wide(up_part), as_wide(up_w))).astype(jnp.bfloat16)
    return (row_grad, inner, gate_wgrad, up_wgrad, down_part)

def slot_scales(selected, filled, source):
    flat = pair_weights(selected).reshape(-1)
    return jnp.where(filled, flat[source], 0.0).astype(jnp.bfloat16)

def source_backward(values, normed, selected, routes, gain, router, slots, row_grad, inner, cot_in):
    top = routes.shape[1]
    experts = router.shape[-1]
    width = values.shape[1]
    pulled = pick_rows(row_grad, slots).reshape(values.shape[0], top, width)
    dnormed = lax.optimization_barrier(jnp.sum(pulled, axis=1))
    dweight = pick_rows(inner, slots).reshape(values.shape[0], top)
    _, pull = jax.vjp(pair_weights, selected)
    dsel = pull(dweight)[0]
    onehot = (routes[:, :, None] == jnp.arange(experts, dtype=jnp.int32)[None, None, :]).astype(jnp.float32)
    dlogits = lax.optimization_barrier(jnp.sum(onehot * dsel[:, :, None], axis=1))
    router_f = router.astype(jnp.float32)
    dnormed = dnormed + jnp.dot(dlogits, router_f.T, precision=lax.Precision.HIGHEST)
    router_part = jnp.dot(normed.astype(jnp.float32).T, dlogits, precision=lax.Precision.HIGHEST)
    _, pull_norm = jax.vjp(rms_scaled, values, gain)
    dvalues, dgain = pull_norm(dnormed)
    grad_in = (cot_in.astype(jnp.float32) + dvalues).astype(jnp.bfloat16)
    return (grad_in, router_part, dgain)

def reference(next_input, prev_input, next_cot, gate_weight, up_weight, down_weight, router, gain, next_routes, prev_routes, next_priority, prev_priority):
    capacity = CAP
    blocks = N_EXPERT
    section_in = jnp.roll(next_input, 1, axis=0)
    cot_all = jnp.roll(next_cot, -1, axis=0)
    outs = ([], [], [], [], [], [], [])
    for section in range(N_PIPE):
        gw, uw, dw = (gate_weight[section], up_weight[section], down_weight[section])
        rw, gn = (router[section], gain[section])

        def prep(x_blk, r_blk, p_blk):
            return prepare(x_blk, gn, rw, r_blk, p_blk, capacity)
        xs = section_in[section].reshape(blocks, TOK_DEV, D)
        values, normed, selected, slots, filled, source, rows = jax.vmap(prep)(xs, next_routes[section].reshape(blocks, TOK_DEV, TOP), next_priority[section].reshape(blocks, TOK_DEV))
        produced = expert_forward(rows, gw, uw, dw)
        forward = jax.vmap(combine)(values, selected, slots, produced)
        outs[0].append(forward.reshape(TOKENS, D))
        xp = prev_input[section].reshape(blocks, TOK_DEV, D)
        proutes = prev_routes[section].reshape(blocks, TOK_DEV, TOP)
        values, normed, selected, slots, filled, source, rows = jax.vmap(prep)(xp, proutes, prev_priority[section].reshape(blocks, TOK_DEV))
        cot_in = cot_all[section].reshape(blocks, TOK_DEV, D)
        token = source // TOP
        cot_rows = jax.vmap(lambda c, f, t: jnp.where(f[:, None], c[t], jnp.zeros_like(c[t])))(cot_in, filled, token)
        cot_rows = cot_rows.reshape(rows.shape)
        scales = jax.vmap(slot_scales)(selected, filled, source).reshape(rows.shape[:3] + (1,))
        row_grad, inner, gate_wgrad, up_wgrad, down_part = expert_backward(rows, cot_rows, scales, gw, uw, dw)

        def finish(v, n, s, r, sl, rg, inn, c):
            return source_backward(v, n, s, r, gn, rw, sl, rg, inn, c)
        grad_in, router_part, dgain = jax.vmap(finish)(values, normed, selected, proutes, slots, row_grad, inner, cot_in)
        outs[1].append(grad_in.reshape(TOKENS, D))
        outs[2].append(gate_wgrad.astype(jnp.bfloat16))
        outs[3].append(up_wgrad.astype(jnp.bfloat16))
        outs[4].append(down_part.astype(jnp.bfloat16))
        outs[5].append(lax.optimization_barrier(jnp.sum(router_part, axis=0)))
        outs[6].append(lax.optimization_barrier(jnp.sum(dgain, axis=0)))
    return (jnp.stack(outs[0]), jnp.stack(outs[1]), jnp.stack(outs[2]), jnp.stack(outs[3]), jnp.stack(outs[4]), jnp.stack(outs[5]), jnp.stack(outs[6]))
```

```python
import functools

import jax
import jax.numpy as jnp
from jax import lax
from jax.experimental import pallas as pl
from jax.experimental.pallas import tpu as pltpu
from jax.sharding import PartitionSpec as P

EPS = 1e-06
MESH = pl.DeviceIdType.MESH
BF = jnp.bfloat16
F32 = jnp.float32
E = 32
T = 256
D = 2048
FF = 768
R = 640
RA = 512
Q = 512


def iota(shape, dim):
    return lax.broadcasted_iota(jnp.int32, shape, dim)


def dot(a, b):
    return jnp.dot(a, b, preferred_element_type=F32)


def dot_nt(a, b):
    return lax.dot_general(a, b, (((1,), (1,)), ((), ())), preferred_element_type=F32)


def halves(a):
    high = a.astype(BF)
    return high, (a - high.astype(F32)).astype(BF)


def cols(i, width):
    return pl.ds(pl.multiple_of(i * width, width), width)


def body(
    nx, cot, gw, uw, dw, xp, router, gain, nroutes, proutes, nprio, pprio,
    fout, gin, ggrad, ugrad, dgrad, rgrad, gaing,
    wg, wu, wd, xin, dyin, rpad, normp, normf,
    sa, sb, sat, sbt, wahi, walo, wbhi, wblo, dlt, prow, perm, permt,
    sx, sxb, sy, syb, sf, sfb, rx, rxb, ry, ryb, rf, rfb,
    gbuf, ubuf, act, gpart, upart, actt, iacc, itile, irecv,
    od, ost, odb, of, ofb, qd, qdb, qf, qfb, dn,
    rps, rrecv, rsum, rall, gsend, grecv,
    wsem, psend, precv, xs, xr, ls, osem,
):
    me = lax.axis_index("expert")
    pipe = lax.axis_index("pipe")
    n_pipe = lax.axis_size("pipe")
    ahead, behind = lax.rem(pipe + 1, n_pipe), lax.rem(pipe + n_pipe - 1, n_pipe)
    mx, mz, my = me // 8, (me // 2) % 4, me % 2

    def peer_of(k):
        return ((mx + k // 8) % 4) * 8 + ((mz + (k // 2) % 4) % 4) * 2 + (my + k % 2) % 2

    loads = [
        pltpu.make_async_copy(src, dst, wsem.at[i])
        for i, (src, dst) in enumerate(((gw, wg), (uw, wu), (dw, wd)))
    ]
    for load in loads:
        load.start()

    barrier = pltpu.get_barrier_semaphore()

    @pl.loop(1, E)
    def _(k):
        pl.semaphore_signal(barrier, 1, device_id={"expert": peer_of(k)}, device_id_type=MESH)

    for other in (ahead, behind):
        pl.semaphore_signal(barrier, 1, device_id={"pipe": other}, device_id_type=MESH)
    pl.semaphore_wait(barrier, E + 1)

    pipes = [
        pltpu.make_async_remote_copy(
            cot, dyin, psend.at[0], precv.at[0], device_id={"pipe": behind}, device_id_type=MESH
        ),
        pltpu.make_async_remote_copy(
            nx, xin, psend.at[1], precv.at[1], device_id={"pipe": ahead}, device_id_type=MESH
        ),
    ]
    for copy in pipes:
        copy.start()

    def send(index, src, dst, rows):
        mine = pl.ds(pl.multiple_of(me * rows, rows), rows)

        @pl.loop(1, E)
        def _(k):
            to = peer_of(k)
            theirs = pl.ds(pl.multiple_of(to * rows, rows), rows)
            pltpu.make_async_remote_copy(
                src.at[theirs], dst.at[mine], xs.at[index], xr.at[index],
                device_id={"expert": to}, device_id_type=MESH,
            ).start()

        pltpu.make_async_copy(src.at[mine], dst.at[mine], ls.at[index]).start()

    def received(index, src, dst, rows):
        mine = pl.ds(pl.multiple_of(me * rows, rows), rows)
        others = pl.ds(0, (E - 1) * rows)
        pltpu.make_async_copy(src.at[others], dst.at[others], xr.at[index]).wait()
        pltpu.make_async_copy(src.at[mine], dst.at[mine], ls.at[index]).wait()

    def sent(index, src, rows):
        others = pl.ds(0, (E - 1) * rows)
        pltpu.make_async_copy(src.at[others], src.at[others], xs.at[index]).wait()

    rpad[...] = jnp.zeros_like(rpad)
    rpad[:, 0:E] = router[...]
    expand = (iota((RA, 128), 0) // 16 == iota((RA, 128), 1)).astype(F32).astype(BF)
    expandt = (iota((128, RA), 1) // 16 == iota((128, RA), 0)).astype(F32).astype(BF)

    def normalise(x, norm):
        @pl.loop(0, T // 64)
        def _(i):
            rows = cols(i, 64)
            v = x[rows, :].astype(F32)
            scale = lax.rsqrt(jnp.sum(v * v, axis=1, keepdims=True) * (1.0 / D) + EPS)
            norm[rows, :] = (v * scale * gain[...]).astype(BF)

    def picks(routes):
        e = iota((128, T), 0)
        return e == routes[0:1, :], e == routes[1:2, :]

    def gates(norm, first, second):
        logits = dot(norm[...], rpad[...]).T
        s0 = jax.nn.sigmoid(jnp.sum(jnp.where(first, logits, 0.0), axis=0, keepdims=True))
        s1 = jax.nn.sigmoid(jnp.sum(jnp.where(second, logits, 0.0), axis=0, keepdims=True))
        total = s0 + s1
        return s0, s1, s0 / total, s1 / total

    def ranks(first, second, prio):
        across = jnp.broadcast_to(prio[...].astype(F32), (T, T))
        before = jnp.where(across.T < across, 1.0, 0.0).astype(BF)
        chosen = jnp.where(first | second, 1.0, 0.0)
        count = dot(chosen.astype(BF), before)
        return jnp.where(first | second, count, -1.0)

    row16 = (iota((RA, T), 0) % 16).astype(F32)
    row4 = (iota((RA, T), 0) % 4).astype(F32) + 16.0
    col16 = (iota((T, RA), 1) % 16).astype(F32)
    col4 = (iota((T, RA), 1) % 4).astype(F32) + 16.0

    def fill(source, a, b, first_a, first_b):
        mask = (iota((RA, T), 0) % 16) // 4

        @pl.loop(0, 4)
        def _(q):
            part = cols(q, Q)
            a[:, part] = dot(first_a[...], source[:, part]).astype(BF)

        total = jnp.zeros((RA, Q), F32)
        picked = first_b[...].astype(F32)
        for q in range(4):
            own = jnp.where(mask == q, picked, 0.0).astype(BF)
            total = total + dot(own, source[:, q * Q : (q + 1) * Q])
        b[:, 0:Q] = total.astype(BF)

    normalise(xp, normp)
    first, second = picks(proutes)
    s0, s1, w0, w1 = gates(normp, first, second)
    prow[0:1, :] = s0
    prow[1:2, :] = s1
    prow[2:3, :] = w0
    prow[3:4, :] = w1
    rank = ranks(first, second, pprio)
    spread = dot(expand, rank.astype(BF))
    take_a = jnp.where(spread == row16, 1.0, 0.0)
    take_b = jnp.where(spread == row4, 1.0, 0.0)
    sa[...] = take_a.astype(BF)
    sb[...] = take_b.astype(BF)
    fill(normp, sx, sxb, sa, sb)
    send(0, sx, rx, 16)
    send(1, sxb, rxb, 16)

    weight = jnp.where(first, w0, 0.0) + jnp.where(second, w1, 0.0)
    spread_w = dot(expand, weight.astype(BF))
    wa = jnp.sum(take_a * spread_w, axis=1, keepdims=True)
    wb = jnp.sum(take_b * spread_w, axis=1, keepdims=True)
    lane = iota((RA, 128), 1)
    syb[:, Q : Q + 128] = jnp.where(lane < 64, wa, wb).astype(BF)
    spread_t = dot(rank.T.astype(BF), expandt)
    sat[...] = jnp.where(spread_t == col16, 1.0, 0.0).astype(BF)
    sbt[...] = jnp.where(spread_t == col4, 1.0, 0.0).astype(BF)
    i0, i1 = iota((RA, RA), 0), iota((RA, RA), 1)
    perm[...] = jnp.where(
        i1 == ((i0 % 128) // 4) * 16 + (i0 // 128) * 4 + i0 % 4, 1.0, 0.0
    ).astype(BF)
    permt[...] = jnp.where(
        i0 == ((i1 % 128) // 4) * 16 + (i1 // 128) * 4 + i1 % 4, 1.0, 0.0
    ).astype(BF)

    pipes[0].wait_recv()
    fill(dyin, sy, syb, sa, sb)
    send(2, sy, ry, 16)
    send(3, syb, ryb, 16)

    pipes[1].wait_recv()
    normalise(xin, normf)
    first, second = picks(nroutes)
    s0, s1, w0, w1 = gates(normf, first, second)
    rank = ranks(first, second, nprio)
    spread = dot(expand, rank.astype(BF))
    wahi[...] = jnp.where(spread == row16, 1.0, 0.0).astype(BF).T
    wbhi[...] = jnp.where(spread == row4, 1.0, 0.0).astype(BF).T
    walo[...] = jnp.zeros_like(walo)
    wblo[...] = jnp.zeros_like(wblo)
    od[0:RA, 0:T] = jnp.where(spread == row16, 1.0, 0.0).astype(BF)
    od[0:RA, T : 2 * T] = jnp.where(spread == row4, 1.0, 0.0).astype(BF)
    fill(normf, sf, sfb, od.at[0:RA, 0:T], od.at[0:RA, T : 2 * T])
    send(4, sf, rf, 16)
    send(5, sfb, rfb, 16)
    weight = jnp.where(first, w0, 0.0) + jnp.where(second, w1, 0.0)
    high, low = halves(weight.T)
    spread_t = dot(rank.T.astype(BF), expandt)
    spread_hi, spread_lo = dot(high, expandt), dot(low, expandt)
    wahi[...] = jnp.where(spread_t == col16, spread_hi, 0.0).astype(BF)
    walo[...] = jnp.where(spread_t == col16, spread_lo, 0.0).astype(BF)
    wbhi[...] = jnp.where(spread_t == col4, spread_hi, 0.0).astype(BF)
    wblo[...] = jnp.where(spread_t == col4, spread_lo, 0.0).astype(BF)

    def unpack(b, x):
        stacked = dot(perm[...], b[:, 0:Q]).astype(BF)
        for q in range(4):
            x[RA:R, q * Q : (q + 1) * Q] = stacked[q * 128 : (q + 1) * 128]

    received(0, sx, rx, 16)
    received(1, sxb, rxb, 16)
    unpack(rxb, rx)
    loads[0].wait()
    loads[1].wait()

    @pl.loop(0, FF // 256)
    def _(n):
        part = cols(n, 256)
        g = dot(rx[...], wg[:, part])
        u = dot(rx[...], wu[:, part])
        gbuf[:, part] = g
        ubuf[:, part] = u
        act[:, part] = (g * jax.nn.sigmoid(g) * u).astype(BF)

    received(2, sy, ry, 16)
    received(3, syb, ryb, 16)
    unpack(ryb, ry)
    loads[2].wait()
    iacc[...] = jnp.zeros_like(iacc)

    @pl.loop(0, 4)
    def _(q):
        part = cols(q, Q)
        result = dot(act[...], wd[:, part]).astype(BF).astype(F32)
        product = result * ry[:, part].astype(F32)
        total = product[:, 0:128]
        for i in range(1, 4):
            total = total + product[:, i * 128 : (i + 1) * 128]
        iacc[...] += total

    inner = jnp.sum(iacc[...], axis=1, keepdims=True).astype(BF).astype(F32)
    inner_b = jnp.broadcast_to(inner[RA:R], (128, 128)).astype(BF)
    placed_b = dot(permt[:, 0:128], inner_b)
    itile[...] = jnp.where(lane < 64, inner[0:RA], placed_b).astype(BF)
    send(6, itile, irecv, 16)

    scale_b = dot(perm[0:128, :], ryb[:, Q : Q + 128])[:, 64:65]
    scale_a = ryb[:, Q : Q + 1].astype(F32)

    @pl.loop(0, 4)
    def _(q):
        part = cols(q, Q)
        ry[0:RA, part] = (ry[0:RA, part].astype(F32) * scale_a).astype(BF)
        ry[RA:R, part] = (ry[RA:R, part].astype(F32) * scale_b).astype(BF)

    @pl.loop(0, FF // 256)
    def _(n):
        part = cols(n, 256)
        back = dot_nt(ry[...], wd[part, :])
        g = gbuf[:, part]
        sig = jax.nn.sigmoid(g)
        gpart[:, part] = (back * ubuf[:, part] * sig * (1.0 + g * (1.0 - sig))).astype(BF)
        upart[:, part] = (back * g * sig).astype(BF)

    def put(out, q, a, stack):
        a[:, cols(q, Q)] = out[0:RA]
        stack[cols(q, 128), :] = out[RA:R]

    @pl.loop(0, 4)
    def _(q):
        part = cols(q, Q)
        out = dot_nt(gpart[...], wg[part, :]) + dot_nt(upart[...], wu[part, :])
        put(out.astype(BF), q, od, ost)

    odb[...] = dot(permt[...], ost[...]).astype(BF)
    send(7, od, qd, 16)
    send(8, odb, qdb, 16)

    received(4, sf, rf, 16)
    received(5, sfb, rfb, 16)
    unpack(rfb, rf)

    @pl.loop(0, FF // 256)
    def _(n):
        part = cols(n, 256)
        g = dot(rf[...], wg[:, part])
        u = dot(rf[...], wu[:, part])
        gbuf[:, part] = g * jax.nn.sigmoid(g) * u

    actf = gbuf[...].astype(BF)

    @pl.loop(0, 4)
    def _(q):
        put(dot(actf, wd[:, cols(q, Q)]).astype(BF), q, of, ost)

    ofb[...] = dot(permt[...], ost[...]).astype(BF)
    send(9, of, qf, 16)
    send(10, ofb, qfb, 16)

    received(6, itile, irecv, 16)
    first, second = picks(proutes)
    mixed = (
        sa[...].astype(F32) * irecv[:, 0:1].astype(F32)
        + sb[...].astype(F32) * irecv[:, 64:65].astype(F32)
    )
    per_expert = dot(expandt, mixed.astype(BF))
    d0 = jnp.sum(jnp.where(first, per_expert, 0.0), axis=0, keepdims=True)
    d1 = jnp.sum(jnp.where(second, per_expert, 0.0), axis=0, keepdims=True)
    s0, s1, w0, w1 = prow[0:1, :], prow[1:2, :], prow[2:3, :], prow[3:4, :]
    shared = w0 * w1 * (d0 - d1)
    dlogits = jnp.where(first, shared * (1.0 - s0), 0.0) - jnp.where(
        second, shared * (1.0 - s1), 0.0
    )
    dlt[...] = dlogits
    high, low = halves(dlogits[0:E])
    both = jnp.concatenate([high, low], axis=0)
    for q in range(4):
        terms = dot(both, normp[:, q * Q : (q + 1) * Q])
        rps[:, q * Q : (q + 1) * Q] = terms[0:E] + terms[E : 2 * E]

    def tile_of(ref, owner):
        return ref.at[
            pl.ds(pl.multiple_of((owner // 8) * 8, 8), 8),
            pl.ds(pl.multiple_of((owner % 8) * 256, 256), 256),
        ]

    mine8 = pl.ds(pl.multiple_of(me * 8, 8), 8)

    @pl.loop(1, E)
    def _(k):
        to = peer_of(k)
        pltpu.make_async_remote_copy(
            tile_of(rps, to), rrecv.at[mine8], xs.at[11], xr.at[11],
            device_id={"expert": to}, device_id_type=MESH,
        ).start()

    pltpu.make_async_copy(tile_of(rps, me), rrecv.at[mine8], ls.at[11]).start()

    actt[...] = act[...].T

    @pl.loop(0, 4)
    def _(q):
        part = cols(q, Q)
        wd[:, part] = dot(actt[...], ry[:, part]).astype(BF)

    stores = [
        pltpu.make_async_copy(src, dst, osem.at[i])
        for i, (src, dst) in enumerate(((wg, ggrad), (wu, ugrad), (wd, dgrad)))
    ]
    stores[2].start()

    @pl.loop(0, 4)
    def _(q):
        part = cols(q, Q)
        turned = rx[:, part].T
        wg[part, :] = dot(turned, gpart[...]).astype(BF)
        wu[part, :] = dot(turned, upart[...]).astype(BF)

    stores[0].start()
    stores[1].start()

    others8 = pl.ds(0, (E - 1) * 8)
    pltpu.make_async_copy(rrecv.at[others8], rrecv.at[others8], xr.at[11]).wait()
    pltpu.make_async_copy(tile_of(rps, me), rrecv.at[mine8], ls.at[11]).wait()
    total = rrecv[0:8, :]
    for i in range(1, E):
        total = total + rrecv[i * 8 : (i + 1) * 8, :]
    rsum[...] = total

    @pl.loop(1, E)
    def _(k):
        pltpu.make_async_remote_copy(
            rsum, tile_of(rall, me), xs.at[12], xr.at[12],
            device_id={"expert": peer_of(k)}, device_id_type=MESH,
        ).start()

    pltpu.make_async_copy(rsum, tile_of(rall, me), ls.at[12]).start()

    received(7, od, qd, 16)
    received(8, odb, qdb, 16)
    dl_high, dl_low = halves(dlt[...].T)
    colq = (iota((T, RA), 1) % 16) // 4

    for q in range(4):
        part = slice(q * Q, (q + 1) * Q)
        own = jnp.where(colq == q, sbt[...].astype(F32), 0.0).astype(BF)
        total = dot(sat[...], qd[:, part]) + dot(own, qdb[...])
        total = total + dot_nt(dl_high, rpad[part, :]) + dot_nt(dl_low, rpad[part, :])
        dn[:, part] = total

    iacc_g = jnp.zeros((1, D), F32)

    def back_norm(i, acc):
        rows = cols(i, 64)
        v = xp[rows, :].astype(F32)
        scale = lax.rsqrt(jnp.sum(v * v, axis=1, keepdims=True) * (1.0 / D) + EPS)
        d = dn[rows, :]
        vs = v * scale
        h = d * gain[...]
        mean = jnp.sum(h * vs, axis=1, keepdims=True) * (1.0 / D)
        gin[rows, :] = (dyin[rows, :].astype(F32) + scale * (h - vs * mean)).astype(BF)
        return acc + jnp.sum(d * vs, axis=0, keepdims=True)

    acc = lax.fori_loop(0, T // 64, back_norm, iacc_g)
    for i in range(16):
        gsend[i : i + 1, :] = acc[:, i * 128 : (i + 1) * 128]
    mine = pl.ds(pl.multiple_of(me * 16, 16), 16)

    @pl.loop(1, E)
    def _(k):
        pltpu.make_async_remote_copy(
            gsend, grecv.at[mine], xs.at[13], xr.at[13],
            device_id={"expert": peer_of(k)}, device_id_type=MESH,
        ).start()

    pltpu.make_async_copy(gsend, grecv.at[mine], ls.at[13]).start()

    received(9, of, qf, 16)
    received(10, ofb, qfb, 16)
    for q in range(4):
        part = slice(q * Q, (q + 1) * Q)
        total = dot(wahi[...], qf[:, part]) + dot(walo[...], qf[:, part])
        for w in (wbhi, wblo):
            own = jnp.where(colq == q, w[...].astype(F32), 0.0).astype(BF)
            total = total + dot(own, qfb[...])
        fout[:, part] = (xin[:, part].astype(F32) + total).astype(BF)

    others16 = pl.ds(0, (E - 1) * 16)
    pltpu.make_async_copy(grecv.at[others16], grecv.at[others16], xr.at[13]).wait()
    pltpu.make_async_copy(gsend, grecv.at[mine], ls.at[13]).wait()
    total = grecv[0:16, :]
    for i in range(1, E):
        total = total + grecv[i * 16 : (i + 1) * 16, :]
    gaing[...] = total

    pltpu.make_async_copy(rrecv.at[others8], rrecv.at[others8], xr.at[12]).wait()
    pltpu.make_async_copy(rsum, tile_of(rall, me), ls.at[12]).wait()
    rgrad[...] = rall[...]

    for copy in pipes:
        copy.wait_send()
    for index, src in (
        (0, sx), (1, sxb), (2, sy), (3, syb), (4, sf), (5, sfb),
        (6, itile), (7, od), (8, odb), (9, of), (10, ofb), (13, grecv),
    ):
        sent(index, src, 16)
    for index in (11, 12):
        sent(index, rrecv, 8)
    for store in stores:
        store.wait()


def per_device(
    next_input, prev_input, next_cot, gate_weight, up_weight, down_weight,
    router, gain, next_routes, prev_routes, next_priority, prev_priority,
):
    anywhere = pl.BlockSpec(memory_space=pl.ANY)
    near = pl.BlockSpec(memory_space=pltpu.VMEM)
    vm = pltpu.VMEM
    grads = [jax.ShapeDtypeStruct(s, BF) for s in ((D, FF), (D, FF), (FF, D))]
    out = pl.pallas_call(
        body,
        name="slot",
        out_shape=[
            jax.ShapeDtypeStruct((T, D), BF),
            jax.ShapeDtypeStruct((T, D), BF),
            *grads,
            jax.ShapeDtypeStruct((E, D), F32),
            jax.ShapeDtypeStruct((16, 128), F32),
        ],
        in_specs=[anywhere] * 5 + [near] * 7,
        out_specs=[near, near, anywhere, anywhere, anywhere, near, near],
        scratch_shapes=[
            vm((D, FF), BF), vm((D, FF), BF), vm((FF, D), BF),
            vm((T, D), BF), vm((T, D), BF), vm((D, 128), BF),
            vm((T, D), BF), vm((T, D), BF),
            vm((RA, T), BF), vm((RA, T), BF), vm((T, RA), BF), vm((T, RA), BF),
            vm((T, RA), BF), vm((T, RA), BF), vm((T, RA), BF), vm((T, RA), BF),
            vm((128, T), F32), vm((8, T), F32),
            vm((RA, RA), BF), vm((RA, RA), BF),
            vm((RA, D), BF), vm((RA, Q), BF),
            vm((RA, D), BF), vm((RA, Q + 128), BF),
            vm((RA, D), BF), vm((RA, Q), BF),
            vm((R, D), BF), vm((RA, Q), BF),
            vm((R, D), BF), vm((RA, Q + 128), BF),
            vm((R, D), BF), vm((RA, Q), BF),
            vm((R, FF), F32), vm((R, FF), F32),
            vm((R, FF), BF), vm((R, FF), BF), vm((R, FF), BF),
            vm((FF, R), BF), vm((R, 128), F32),
            vm((RA, 128), BF), vm((RA, 128), BF),
            vm((RA, D), BF), vm((RA, Q), BF), vm((RA, Q), BF),
            vm((RA, D), BF), vm((RA, Q), BF),
            vm((RA, D), BF), vm((RA, Q), BF),
            vm((RA, D), BF), vm((RA, Q), BF),
            vm((T, D), F32),
            vm((E, D), F32), vm((256, 256), F32), vm((8, 256), F32), vm((E, D), F32),
            vm((16, 128), F32), vm((RA, 128), F32),
            pltpu.SemaphoreType.DMA((3,)),
            pltpu.SemaphoreType.DMA((2,)), pltpu.SemaphoreType.DMA((2,)),
            pltpu.SemaphoreType.DMA((14,)), pltpu.SemaphoreType.DMA((14,)),
            pltpu.SemaphoreType.DMA((14,)), pltpu.SemaphoreType.DMA((3,)),
        ],
        compiler_params=pltpu.CompilerParams(
            collective_id=0, has_side_effects=True, vmem_limit_bytes=67_000_000
        ),
    )(
        next_input[0], next_cot[0], gate_weight[0, 0], up_weight[0, 0], down_weight[0, 0],
        prev_input[0], router[0], gain, next_routes[0].T, prev_routes[0].T,
        next_priority, prev_priority,
    )
    fout, gin, gg, ug, dg, rg, gaing = out
    return (
        fout[None], gin[None], gg[None, None], ug[None, None], dg[None, None],
        rg.T[None], gaing.reshape(1, D),
    )


def solution(mesh):
    tokens = P("pipe", "expert", None)
    experts = P("pipe", "expert", None, None)
    return jax.shard_map(
        per_device,
        mesh=mesh,
        in_specs=(
            tokens, tokens, tokens, experts, experts, experts,
            P("pipe", None, None), P("pipe", None), tokens, tokens,
            P("pipe", "expert"), P("pipe", "expert"),
        ),
        out_specs=(
            tokens, tokens, experts, experts, experts,
            P("pipe", None, None), P("pipe", None),
        ),
        check_vma=False,
    )
```
